32 devices in a mesh: grp: 2 (over x), row: 8 (over z, y), col: 2 (over core).
Axes of the slice: x: 2, y: 2, z: 4, core: 2. Of those that a mesh axis runs over, the one named last changes fastest.
Arguments:
- pair_act: bfloat16 [64, 32, 128], P(('grp', 'row'), 'col'), parts along dimension 0, may hold values from -200 to 200
- cotangent: bfloat16 [64, 32, 128], P(('grp', 'row'), 'col'), parts along dimension 0, may hold values from -6 to 6
- residue_mask: int32 [64], P('grp'), parts along dimension 0, may hold values from 0 to 1, as said below
- front_weight: bfloat16 [2, 128, 640], replicated, may hold values from -0.5 to 0.5
- out_weight: bfloat16 [2, 128, 128], replicated, may hold values from -0.5 to 0.5
Outputs:
- pair_grad: bfloat16 [64, 32, 128], P(('grp', 'row'), 'col'), parts along dimension 0
The draws below stay inside these ranges and needn't reach their ends.
There are 2 independent parts, one for each index of `grp`. The reference program is written for one: setup_inputs(seed, part) draws one part's arguments, and reference() takes and returns one part's arrays. A program takes and returns all parts, laid end to end along the dimension named above; an argument that names none is the same for every part. Nothing has to cross between parts.
Inputs may be any that keep to these rules, and one draw needn't show every extreme that they name: residue_mask is 1 on residues 0 to L - 1 and 0 from L on, for a chain length L of at least 24.
All inputs are finite; a program needn't handle non-finite values.
Results may differ from the reference program's by a relative error of at most 0.01.
Values may be sent and summed in bfloat16 or wider, within the bound.
A program may use at most 64 MiB of HBM per device.

```python
import math
import jax
import jax.numpy as jnp
from jax import lax

C = 128
H = 128
N = 32


def draw_pair_act(key, part):
    keys = jax.random.split(jax.random.fold_in(key, 11), 3)
    base = jax.random.normal(keys[0], (N, N, C), jnp.float32)
    cell_scale = jnp.exp(jax.random.uniform(keys[1], (N, N, 1), jnp.float32, 0.0, math.log(10.0)))
    channel_scale = jnp.exp(jax.random.uniform(keys[2], (1, 1, C), jnp.float32, 0.0, math.log(10.0)))
    values = base * channel_scale * cell_scale
    return jnp.clip(values / 3.0, -200.0, 200.0).astype(jnp.bfloat16)


def draw_residue_mask(key, part):
    lowest = (3 * N + 3) // 4
    span_len = N - lowest + 1
    offset = jax.random.randint(jax.random.fold_in(key, 23), (), 0, span_len)
    length = lowest + (offset + jnp.asarray(part, jnp.int32)) % span_len
    return (jnp.arange(N, dtype=jnp.int32) < length).astype(jnp.int32)


def block_levels(key, dims, shards, least, high):
    factor_of, own = 1.0, jax.random.fold_in(key, 6)
    for position, parts in shards:
        heights = jnp.exp(jax.random.uniform(jax.random.fold_in(own, position), (parts,), jnp.float32, least / len(shards), high / len(shards)))
        factor_of = factor_of * jnp.repeat(heights, dims[position] // parts).reshape([-1 if axis == position else 1 for axis in range(len(dims))])
    return factor_of


def bell_draw(own_key, extent, scale, limit, pieces=(), kind=jnp.bfloat16):
    factor_of = block_levels(own_key, extent, pieces, -0.22, 0.18) if pieces else 1.0
    array = jax.random.normal(own_key, extent, jnp.float32) * scale * factor_of
    return jnp.minimum(jnp.maximum(array, -limit), limit).astype(kind)


def setup_inputs(seed: int = 0, part: int = 0) -> dict:
    seeds = jax.random.split(jax.random.key(seed), 6)
    own_keys = jax.random.split(jax.random.fold_in(seeds[5], part), 6)
    pair_act = draw_pair_act(jax.random.fold_in(jax.random.fold_in(seeds[5], part), 71), part)
    cotangent = bell_draw(own_keys[1], (N, N, C), 1.0, 6.0, ((0, 8), (1, 2)))
    residue_mask = draw_residue_mask(jax.random.fold_in(jax.random.fold_in(seeds[5], part), 71), part)
    front_weight = bell_draw(seeds[3], (2, C, 4 * H + C), C ** -0.5, 0.5)
    out_weight = bell_draw(seeds[4], (2, H, C), H ** -0.5, 0.5)
    return dict(pair_act=pair_act, cotangent=cotangent, residue_mask=residue_mask, front_weight=front_weight, out_weight=out_weight)


def layer_norm(values):
    centred = values - lax.optimization_barrier(jnp.mean(values, axis=-1, keepdims=True))
    spread = lax.optimization_barrier(jnp.mean(centred * centred, axis=-1, keepdims=True))
    return centred * lax.rsqrt(spread + 1e-05)

def project_pair(inner_pair, mask_pair, weight):
    normed = layer_norm(inner_pair.astype(jnp.float32)).astype(jnp.bfloat16)
    linear = jnp.dot(normed, weight, preferred_element_type=jnp.float32)
    left_side = jax.nn.sigmoid(linear[..., :H]) * linear[..., H:2 * H]
    right_side = jax.nn.sigmoid(linear[..., 2 * H:3 * H]) * linear[..., 3 * H:4 * H]
    operands = (jnp.stack((left_side, right_side)) * mask_pair[None, :, :, None]).astype(jnp.bfloat16)
    return (operands, jax.nn.sigmoid(linear[..., 4 * H:]))

def finish(mixed_part, gate_value, inner_pair, weight):
    normed = layer_norm(mixed_part).astype(jnp.bfloat16)
    update = jnp.dot(normed, weight, preferred_element_type=jnp.float32)
    return (inner_pair.astype(jnp.float32) + gate_value * update).astype(jnp.bfloat16)

def rounded(values):
    return lax.optimization_barrier(values.astype(jnp.bfloat16)).astype(jnp.float32)

def reference(pair_act, cotangent, residue_mask, front_weight, out_weight):
    chain_mask = residue_mask.astype(jnp.float32)
    mask_pair = chain_mask[:, None] * chain_mask[None, :]
    (out_ops, out_gate), out_front_back = jax.vjp(lambda inner_pair: project_pair(inner_pair, mask_pair, front_weight[0]), pair_act)
    out_left = out_ops[0].astype(jnp.float32)
    out_right = out_ops[1].astype(jnp.float32)
    out_mixed = jnp.einsum('ikc,jkc->ijc', out_left, out_right)
    pair_mid, out_finish_back = jax.vjp(lambda mixed_part, gate_value, inner_pair: finish(mixed_part, gate_value, inner_pair, out_weight[0]), out_mixed, out_gate, pair_act)
    (in_ops, in_gate), in_front_back = jax.vjp(lambda inner_pair: project_pair(inner_pair, mask_pair, front_weight[1]), pair_mid)
    in_left = in_ops[0].astype(jnp.float32)
    in_right = in_ops[1].astype(jnp.float32)
    in_mixed = jnp.einsum('kic,kjc->ijc', in_left, in_right)
    unused_pair, in_finish_back = jax.vjp(lambda mixed_part, gate_value, inner_pair: finish(mixed_part, gate_value, inner_pair, out_weight[1]), in_mixed, in_gate, pair_mid)
    grad_mixed, grad_gate, grad_inner = in_finish_back(cotangent)
    signal = rounded(grad_mixed)
    grad_left = jnp.einsum('ijc,kjc->kic', signal, in_right)
    grad_right = jnp.einsum('ijc,kic->kjc', signal, in_left)
    grad_front, = in_front_back((jnp.stack((grad_left, grad_right)).astype(jnp.bfloat16), grad_gate))
    grad_mid = (grad_inner.astype(jnp.float32) + grad_front.astype(jnp.float32)).astype(jnp.bfloat16)
    grad_mixed, grad_gate, grad_inner = out_finish_back(grad_mid)
    signal = rounded(grad_mixed)
    grad_left = jnp.einsum('ijc,jkc->ikc', signal, out_right)
    grad_right = jnp.einsum('ijc,ikc->jkc', signal, out_left)
    grad_front, = out_front_back((jnp.stack((grad_left, grad_right)).astype(jnp.bfloat16), grad_gate))
    return (grad_inner.astype(jnp.float32) + grad_front.astype(jnp.float32)).astype(jnp.bfloat16)
```

```python
import functools

import jax
import jax.numpy as jnp
from jax import lax
from jax.experimental import pallas as pl
from jax.experimental.pallas import tpu as pltpu
from jax.sharding import PartitionSpec as P

H = 128
TILE = 8
F32 = jnp.float32
BF16 = jnp.bfloat16
MESH = pl.DeviceIdType.MESH
VMEM_BUDGET = 24 << 20
FULL_ARRAYS = 16


def sigmoid(x):
    return 0.5 * jnp.tanh(0.5 * x) + 0.5


def norm(v):
    centred = v - jnp.mean(v, axis=-1, keepdims=True)
    r = lax.rsqrt(jnp.mean(centred * centred, axis=-1, keepdims=True) + 1e-05)
    return centred * r, r


def norm_back(y, r, d):
    return r * (d - jnp.mean(d, axis=-1, keepdims=True) - y * jnp.mean(d * y, axis=-1, keepdims=True))


def rounded(v):
    return v.astype(BF16).astype(F32)


def dot(a, b):
    return jnp.dot(a.astype(BF16), b, preferred_element_type=F32)


def dot_t(a, b):
    return lax.dot_general(
        a.astype(BF16), b, (((1,), (1,)), ((), ())), preferred_element_type=F32
    )


def part(p, n):
    return p[:, n * H : (n + 1) * H]


def flip(value, other, bits):
    total = 0
    for b in range(bits):
        w = 1 << b
        total = total + (value // w + other // w) % 2 * w
    return total


def front_back(x, mask, weight, d_a, d_b, d_gate):
    y, r = norm(x)
    p = dot(y, weight)
    s0, s2, s4 = sigmoid(part(p, 0)), sigmoid(part(p, 2)), sigmoid(part(p, 4))
    ma, mb = d_a * mask * s0, d_b * mask * s2
    d = jnp.concatenate(
        [
            (v.astype(BF16))
            for v in (
                ma * part(p, 1) * (1.0 - s0),
                ma,
                mb * part(p, 3) * (1.0 - s2),
                mb,
                d_gate * s4 * (1.0 - s4),
            )
        ],
        axis=1,
    )
    return rounded(norm_back(y, r, rounded(dot_t(d, weight))))


def crop_kernel(
    rows, pair, cot, mask_in, wf_in, wo_in, out,
    x_all, ct_all, wf, wo, mask, left, right, flipped, mixed, gate, mid,
    in_left, in_right, in_mixed, in_gate, sig, d_left, d_right, ct32, out_sig, grad,
    local_sem, send_sem, recv_sem, fsend_sem, frecv_sem,
):
    n, c = left.shape[0], left.shape[2]
    lr, lc = out.shape[0], out.shape[1]
    bits = rows.bit_length() - 1
    me, my_col = lax.axis_index("row"), lax.axis_index("col")
    other = 1 - my_col
    r0 = pl.multiple_of(me * lr, lr)
    c0 = pl.multiple_of(my_col * lc, lc)

    weights = [
        pltpu.make_async_copy(wf_in, wf, local_sem.at[2]),
        pltpu.make_async_copy(wo_in, wo, local_sem.at[3]),
    ]
    own = []
    for t, (src, dst) in enumerate(((pair, x_all), (cot, ct_all))):
        own.append(
            pltpu.make_async_copy(src, dst.at[pl.ds(r0, lr), pl.ds(c0, lc)], local_sem.at[t])
        )
    for copy in own + weights:
        copy.start()

    barrier = pltpu.get_barrier_semaphore()
    for d in range(1, rows):
        pl.semaphore_signal(
            barrier, inc=1, device_id={"row": flip(me, d, bits)}, device_id_type=MESH
        )
    pl.semaphore_signal(barrier, inc=1, device_id={"col": other}, device_id_type=MESH)

    span = jnp.broadcast_to(mask_in[...].astype(F32), (n, n))
    here = lax.broadcasted_iota(jnp.int32, (n, n), 0) == lax.broadcasted_iota(jnp.int32, (n, n), 1)
    along = jnp.broadcast_to(
        jnp.sum(jnp.where(here, span, 0.0), axis=1, keepdims=True), (n, c)
    )
    flipped[0] = along

    def fill_mask(i, carry):
        mask[i] = along * flipped[0, pl.ds(i, 1), :]
        return carry

    lax.fori_loop(0, n, fill_mask, 0)
    pl.semaphore_wait(barrier, rows)

    def block(ref, row, col):
        return ref.at[
            pl.ds(pl.multiple_of(row * lr, lr), lr), pl.ds(pl.multiple_of(col * lc, lc), lc)
        ]

    def direct(t, d):
        src, dst = ((pair, x_all), (cot, ct_all))[t]
        return pltpu.make_async_remote_copy(
            src_ref=src,
            dst_ref=block(dst, me, my_col),
            send_sem=send_sem.at[t, d],
            recv_sem=recv_sem.at[t, d],
            device_id={"row": flip(me, d, bits)},
            device_id_type=MESH,
        )

    def first(t):
        src, dst = ((pair, x_all), (cot, ct_all))[t]
        return pltpu.make_async_remote_copy(
            src_ref=src,
            dst_ref=block(dst, me, my_col),
            send_sem=fsend_sem.at[t, 0],
            recv_sem=frecv_sem.at[t, 0],
            device_id={"col": other},
            device_id_type=MESH,
        )

    def forward(t, d):
        ref = (x_all, ct_all)[t]
        held = block(ref, flip(me, d, bits), my_col)
        return pltpu.make_async_remote_copy(
            src_ref=held,
            dst_ref=held,
            send_sem=fsend_sem.at[t, d],
            recv_sem=frecv_sem.at[t, d],
            device_id={"col": other},
            device_id_type=MESH,
        )

    def loop(count, step, start=0):
        def body(k, carry):
            step(k)
            return carry

        lax.fori_loop(start, count, body, 0)

    for t in range(2):
        first(t).start()
        loop(rows, lambda d: direct(t, d).start(), 1)

    for copy in weights:
        copy.wait()
    own[0].wait()

    def rows_of(ref, k0, nk):
        return ref[pl.ds(k0, nk)].reshape(nk * n, c)

    def put(ref, k0, nk, v):
        ref[pl.ds(k0, nk)] = v.reshape(nk, n, c)

    def projected(x, k0, nk, weight, a_ref, b_ref, g_ref):
        y, _ = norm(x)
        p = dot(y, weight)
        m = rows_of(mask, k0, nk)
        put(a_ref, k0, nk, rounded(sigmoid(part(p, 0)) * part(p, 1) * m))
        put(b_ref, k0, nk, rounded(sigmoid(part(p, 2)) * part(p, 3) * m))
        put(g_ref, k0, nk, sigmoid(part(p, 4)))

    def front_step(d):
        @pl.when(d + 1 < rows)
        def _():
            direct(0, d + 1).wait_recv()
            forward(0, d + 1).start()

        forward(0, d).wait_recv()
        k0 = flip(me, d, bits) * lr
        projected(rows_of(x_all, k0, lr).astype(F32), k0, lr, wf[0], left, right, gate)

    loop(rows, front_step)

    def transpose(src):
        def step(b):
            i = pl.multiple_of(b * TILE, TILE)
            flipped[:, pl.ds(i, TILE), :] = jnp.swapaxes(src[pl.ds(i, TILE)], 0, 1)

        loop(n // TILE, step)

    def triangle(count, width, row_at, tile_at, store, group):
        def step(b):
            def term(q, acc):
                t = tile_at(q)
                return tuple(v + row_at(b * group + a, q) * t for a, v in enumerate(acc))

            zero = jnp.zeros((width, c), F32)
            acc = lax.fori_loop(0, n, term, (zero,) * group, unroll=True)
            for a in range(group):
                store(b * group + a, acc[a])

        loop(count // group, step)

    transpose(right)

    def put_row(ref):
        def store(a, v):
            ref[a] = v

        return store

    triangle(
        n, n,
        lambda i, k: left[i, pl.ds(k, 1), :],
        lambda k: flipped[k],
        put_row(mixed), 4,
    )

    own[1].wait()

    def pass_on(d):
        direct(1, d).wait_recv()
        forward(1, d).start()

    loop(rows, pass_on, 1)

    def middle_step(b):
        k0 = b * lr
        z, _ = norm(rows_of(mixed, k0, lr))
        x = rows_of(x_all, k0, lr).astype(F32)
        x = rounded(x + rows_of(gate, k0, lr) * dot(z, wo[0]))
        put(mid, k0, lr, x)
        projected(x, k0, lr, wf[1], in_left, in_right, in_gate)

    loop(rows, middle_step)

    triangle(
        n, n,
        lambda i, k: in_left[k, pl.ds(i, 1), :],
        lambda k: in_right[k],
        put_row(in_mixed), 4,
    )

    loop(rows, lambda d: forward(1, d).wait_recv())

    def signal_step(b):
        k0 = b * lr
        z, r = norm(rows_of(in_mixed, k0, lr))
        ct = rows_of(ct_all, k0, lr).astype(F32)
        put(ct32, k0, lr, ct)
        dz = rounded(dot_t(ct * rows_of(in_gate, k0, lr), wo[1]))
        put(sig, k0, lr, rounded(norm_back(z, r, dz)))

    loop(rows, signal_step)
    transpose(sig)

    def strip(k0, nk, j0, width, group, chunk):
        def take(ref, k, m):
            return ref[pl.ds(k, m), pl.ds(j0, width), :].reshape(m * width, c)

        def give(ref, k, m, v):
            ref[pl.ds(k, m), pl.ds(j0, width), :] = v.reshape(m, width, c)

        def into(ref):
            def store(a, v):
                ref[k0 + a, pl.ds(j0, width), :] = rounded(v)

            return store

        triangle(
            nk, width,
            lambda a, j: in_right[k0 + a, pl.ds(j, 1), :],
            lambda j: flipped[j, pl.ds(j0, width), :],
            into(d_left), group,
        )
        triangle(
            nk, width,
            lambda a, i: in_left[k0 + a, pl.ds(i, 1), :],
            lambda i: sig[i, pl.ds(j0, width), :],
            into(d_right), group,
        )

        def back(b):
            k = k0 + b * chunk
            ct = take(ct32, k, chunk)
            z1, _ = norm(take(in_mixed, k, chunk))
            d_in = front_back(
                take(mid, k, chunk), take(mask, k, chunk), wf[1],
                take(d_left, k, chunk), take(d_right, k, chunk),
                ct * dot(z1, wo[1]),
            )
            g = rounded(ct + d_in)
            z0, r = norm(take(mixed, k, chunk))
            dz = rounded(dot_t(g * take(gate, k, chunk), wo[0]))
            give(grad, k, chunk, g)
            give(out_sig, k, chunk, rounded(norm_back(z0, r, dz)))

        loop(nk // chunk, back)

    t0 = pl.multiple_of(me * lr // TILE * TILE, TILE)
    strip(r0, lr, 0, n, lr, lr)
    strip(0, n, t0, max(TILE, lr), TILE, TILE)

    def own_of(ref):
        def store(a, v):
            ref[r0 + a, pl.ds(c0, lc), :] = rounded(v)

        return store

    triangle(
        lr, lc,
        lambda a, j: out_sig[r0 + a, pl.ds(j, 1), :],
        lambda j: right[j, pl.ds(c0, lc), :],
        own_of(d_left), lr,
    )
    triangle(
        lr, lc,
        lambda a, i: out_sig[i, pl.ds(r0 + a, 1), :],
        lambda i: left[i, pl.ds(c0, lc), :],
        own_of(d_right), lr,
    )

    def mine(ref):
        return ref[pl.ds(r0, lr), pl.ds(c0, lc), :].reshape(lr * lc, c)

    z0, _ = norm(mine(mixed))
    g = mine(grad)
    d_front = front_back(
        mine(x_all).astype(F32), mine(mask), wf[0], mine(d_left), mine(d_right),
        g * dot(z0, wo[0]),
    )
    out[...] = (g + d_front).astype(BF16).reshape(lr, lc, c)

    for t in range(2):
        first(t).wait_send()

        def sent(d):
            direct(t, d).wait_send()
            forward(t, d).wait_send()

        loop(rows, sent, 1)


def from_root(array, axis, root):
    mine = lax.axis_index(axis) == root
    return lax.psum(jnp.where(mine, array, jnp.zeros_like(array)), axis)


def layer_norm(values):
    centred = values - jnp.mean(values, axis=-1, keepdims=True)
    spread = jnp.mean(centred * centred, axis=-1, keepdims=True)
    return centred * lax.rsqrt(spread + 1e-05)


def project_pair(inner_pair, mask_pair, weight):
    normed = layer_norm(inner_pair.astype(jnp.float32)).astype(jnp.bfloat16)
    linear = jnp.dot(normed, weight, preferred_element_type=jnp.float32)
    left_side = jax.nn.sigmoid(linear[..., :H]) * linear[..., H : 2 * H]
    right_side = jax.nn.sigmoid(linear[..., 2 * H : 3 * H]) * linear[..., 3 * H : 4 * H]
    operands = (jnp.stack((left_side, right_side)) * mask_pair[None, :, :, None]).astype(
        jnp.bfloat16
    )
    return (operands, jax.nn.sigmoid(linear[..., 4 * H :]))


def finish(mixed_part, gate_value, inner_pair, weight):
    normed = layer_norm(mixed_part).astype(jnp.bfloat16)
    update = jnp.dot(normed, weight, preferred_element_type=jnp.float32)
    return (inner_pair.astype(jnp.float32) + gate_value * update).astype(jnp.bfloat16)


def body(pair_act, cotangent, residue_mask, front_weight, out_weight):
    local_rows = pair_act.shape[0]
    local_cols = pair_act.shape[1]
    row_index = lax.axis_index("row")
    col_index = lax.axis_index("col")
    block_rows = lax.axis_size("row") // lax.axis_size("col")
    owner_col = row_index // block_rows
    offset = row_index % block_rows * local_rows
    chain_mask = residue_mask.astype(jnp.float32)
    mask_rows = lax.dynamic_slice_in_dim(chain_mask, row_index * local_rows, local_rows)
    mask_cols = lax.dynamic_slice_in_dim(chain_mask, col_index * local_cols, local_cols)
    mask_pair = mask_rows[:, None] * mask_cols[None, :]

    def gather_rows(stacked):
        return lax.all_gather(stacked, "row", axis=1, tiled=True)

    def column_block(gathered):
        slab = lax.dynamic_slice_in_dim(gathered, offset, local_rows, 1)
        return from_root(slab, "col", owner_col)

    def gather_cols(values):
        return lax.all_gather(values, "col", axis=1, tiled=True)

    def sum_cols(partial_term):
        return lax.psum_scatter(
            partial_term.astype(jnp.bfloat16), "col", scatter_dimension=1, tiled=True
        ).astype(jnp.float32)

    (out_ops, out_gate), out_front_back = jax.vjp(
        lambda inner_pair: project_pair(inner_pair, mask_pair, front_weight[0]), pair_act
    )
    fetched = gather_rows(out_ops)
    out_mixed = sum_cols(
        jnp.einsum("ikc,jkc->ijc", out_ops[0], fetched[-1], preferred_element_type=jnp.float32)
    )
    pair_mid, out_finish_back = jax.vjp(
        lambda mixed_part, gate_value, inner_pair: finish(
            mixed_part, gate_value, inner_pair, out_weight[0]
        ),
        out_mixed,
        out_gate,
        pair_act,
    )
    (in_ops, in_gate), in_front_back = jax.vjp(
        lambda inner_pair: project_pair(inner_pair, mask_pair, front_weight[1]), pair_mid
    )
    in_fetched = gather_rows(in_ops)
    left_block = column_block(in_fetched[0])
    in_mixed = jnp.einsum(
        "kic,kjc->ijc", left_block, in_fetched[1], preferred_element_type=jnp.float32
    )
    unused_pair, in_finish_back = jax.vjp(
        lambda mixed_part, gate_value, inner_pair: finish(
            mixed_part, gate_value, inner_pair, out_weight[1]
        ),
        in_mixed,
        in_gate,
        pair_mid,
    )
    grad_mixed, grad_gate, grad_inner = in_finish_back(cotangent)
    signal = grad_mixed.astype(jnp.bfloat16)
    signal_rows = gather_rows(signal[None])[0]
    left_rows = gather_cols(in_ops[0])
    grad_right = jnp.einsum(
        "kic,ijc->kjc", left_rows, signal_rows, preferred_element_type=jnp.float32
    )
    grad_left = sum_cols(
        jnp.einsum("kjc,ijc->kic", in_ops[1], signal_rows, preferred_element_type=jnp.float32)
    )
    (grad_front,) = in_front_back(
        (jnp.stack((grad_left, grad_right)).astype(jnp.bfloat16), grad_gate)
    )
    grad_mid = (grad_inner.astype(jnp.float32) + grad_front.astype(jnp.float32)).astype(
        jnp.bfloat16
    )
    grad_mixed, grad_gate, grad_inner = out_finish_back(grad_mid)
    signal = grad_mixed.astype(jnp.bfloat16)
    signal_cols = gather_cols(signal)
    grad_left = jnp.einsum(
        "ijc,jkc->ikc", signal_cols, fetched[-1], preferred_element_type=jnp.float32
    )
    signal_block = column_block(gather_rows(signal[None])[0])
    grad_right = jnp.einsum(
        "ijc,ikc->jkc", signal_block, fetched[0], preferred_element_type=jnp.float32
    )
    (grad_front,) = out_front_back(
        (jnp.stack((grad_left, grad_right)).astype(jnp.bfloat16), grad_gate)
    )
    return (grad_inner.astype(jnp.float32) + grad_front.astype(jnp.float32)).astype(jnp.bfloat16)


def crop_body(rows, pair_act, cotangent, residue_mask, front_weight, out_weight):
    lr, lc, c = pair_act.shape
    n = residue_mask.shape[0]
    full = pltpu.VMEM((n, n, c), F32)
    dma = pltpu.SemaphoreType.DMA
    hbm = pl.BlockSpec(memory_space=pl.ANY)
    return pl.pallas_call(
        functools.partial(crop_kernel, rows),
        out_shape=jax.ShapeDtypeStruct((lr, lc, c), BF16),
        in_specs=[hbm, hbm, pl.BlockSpec(memory_space=pltpu.VMEM), hbm, hbm],
        out_specs=pl.BlockSpec(memory_space=pltpu.VMEM),
        scratch_shapes=[
            pltpu.VMEM((n, n, c), BF16),
            pltpu.VMEM((n, n, c), BF16),
            pltpu.VMEM(front_weight.shape, BF16),
            pltpu.VMEM(out_weight.shape, BF16),
        ]
        + [full] * 17
        + [dma((4,)), dma((2, rows)), dma((2, rows)), dma((2, rows)), dma((2, rows))],
        compiler_params=pltpu.CompilerParams(
            collective_id=0, has_side_effects=True, vmem_limit_bytes=48 << 20
        ),
    )(pair_act, cotangent, residue_mask.reshape(1, n), front_weight, out_weight)


def fits(mesh, n, lr, lc, c):
    rows, cols = mesh.shape["row"], mesh.shape["col"]
    return (
        cols == 2
        and rows & (rows - 1) == 0
        and n % TILE == 0
        and (lr % TILE == 0 or TILE % lr == 0)
        and lc % (2 * TILE) == 0
        and FULL_ARRAYS * 4 * n * n * c <= VMEM_BUDGET
    )


def solution(mesh):
    def dispatch(pair_act, cotangent, residue_mask, front_weight, out_weight):
        n = residue_mask.shape[0]
        if fits(mesh, n, *pair_act.shape):
            return crop_body(
                mesh.shape["row"], pair_act, cotangent, residue_mask, front_weight, out_weight
            )
        return body(pair_act, cotangent, residue_mask, front_weight, out_weight)

    placed = (P(("grp", "row"), "col", None), P(("grp", "row"), "col", None), P("grp"), P(), P())
    return jax.shard_map(
        dispatch,
        mesh=mesh,
        in_specs=placed,
        out_specs=P(("grp", "row"), "col", None),
        check_vma=False,
    )
```

```python
import functools

import jax
import jax.numpy as jnp
from jax import lax
from jax.experimental import pallas as pl
from jax.experimental.pallas import tpu as pltpu
from jax.sharding import PartitionSpec as P

H = 128
TILE = 8
F32 = jnp.float32
BF16 = jnp.bfloat16
MESH = pl.DeviceIdType.MESH
VMEM_BUDGET = 24 << 20
FULL_ARRAYS = 16


def sigmoid(x):
    return 0.5 * jnp.tanh(0.5 * x) + 0.5


def norm(v):
    centred = v - jnp.mean(v, axis=-1, keepdims=True)
    r = lax.rsqrt(jnp.mean(centred * centred, axis=-1, keepdims=True) + 1e-05)
    return centred * r, r


def norm_back(y, r, d):
    return r * (d - jnp.mean(d, axis=-1, keepdims=True) - y * jnp.mean(d * y, axis=-1, keepdims=True))


def rounded(v):
    return v.astype(BF16).astype(F32)


def dot(a, b):
    return jnp.dot(a.astype(BF16), b, preferred_element_type=F32)


def dot_t(a, b):
    return lax.dot_general(
        a.astype(BF16), b, (((1,), (1,)), ((), ())), preferred_element_type=F32
    )


def part(p, n):
    return p[:, n * H : (n + 1) * H]


def flip(value, other, bits):
    total = 0
    for b in range(bits):
        w = 1 << b
        total = total + (value // w + other // w) % 2 * w
    return total


def front_back(x, mask, weight, d_a, d_b, d_gate):
    y, r = norm(x)
    p = dot(y, weight)
    s0, s2, s4 = sigmoid(part(p, 0)), sigmoid(part(p, 2)), sigmoid(part(p, 4))
    ma, mb = d_a * mask * s0, d_b * mask * s2
    d = jnp.concatenate(
        [
            (v.astype(BF16))
            for v in (
                ma * part(p, 1) * (1.0 - s0),
                ma,
                mb * part(p, 3) * (1.0 - s2),
                mb,
                d_gate * s4 * (1.0 - s4),
            )
        ],
        axis=1,
    )
    return rounded(norm_back(y, r, rounded(dot_t(d, weight))))


def crop_kernel(
    rows, pair, cot, mask_in, wf_in, wo_in, out,
    x_all, ct_all, wf, wo, chain, mask, left, right, flipped, mixed, gate, mid,
    in_left, in_right, in_mixed, in_gate, sig, d_left, d_right, ct32, out_sig, grad,
    local_sem, send_sem, recv_sem, fsend_sem, frecv_sem,
):
    n, c = left.shape[0], left.shape[2]
    lr, lc = out.shape[0], out.shape[1]
    bits = rows.bit_length() - 1
    me, my_col = lax.axis_index("row"), lax.axis_index("col")
    other = 1 - my_col
    r0 = pl.multiple_of(me * lr, lr)
    c0 = pl.multiple_of(my_col * lc, lc)

    weights = [
        pltpu.make_async_copy(wf_in, wf, local_sem.at[2]),
        pltpu.make_async_copy(wo_in, wo, local_sem.at[3]),
    ]
    own = []
    for t, (src, dst) in enumerate(((pair, x_all), (cot, ct_all))):
        own.append(
            pltpu.make_async_copy(src, dst.at[pl.ds(r0, lr), pl.ds(c0, lc)], local_sem.at[t])
        )
    chain_copy = pltpu.make_async_copy(mask_in, chain, local_sem.at[4])
    for copy in [chain_copy] + own + weights:
        copy.start()

    barrier = pltpu.get_barrier_semaphore()
    for d in range(1, rows):
        pl.semaphore_signal(
            barrier, inc=1, device_id={"row": flip(me, d, bits)}, device_id_type=MESH
        )
    pl.semaphore_signal(barrier, inc=1, device_id={"col": other}, device_id_type=MESH)

    chain_copy.wait()
    span = jnp.broadcast_to(chain[...].astype(F32), (n, n))
    here = lax.broadcasted_iota(jnp.int32, (n, n), 0) == lax.broadcasted_iota(jnp.int32, (n, n), 1)
    along = jnp.broadcast_to(
        jnp.sum(jnp.where(here, span, 0.0), axis=1, keepdims=True), (n, c)
    )
    flipped[0] = along

    def fill_mask(i, carry):
        mask[i] = along * flipped[0, pl.ds(i, 1), :]
        return carry

    lax.fori_loop(0, n, fill_mask, 0)
    pl.semaphore_wait(barrier, rows)

    def block(ref, row, col):
        return ref.at[
            pl.ds(pl.multiple_of(row * lr, lr), lr), pl.ds(pl.multiple_of(col * lc, lc), lc)
        ]

    def direct(t, d):
        src, dst = ((pair, x_all), (cot, ct_all))[t]
        return pltpu.make_async_remote_copy(
            src_ref=src,
            dst_ref=block(dst, me, my_col),
            send_sem=send_sem.at[t, d],
            recv_sem=recv_sem.at[t, d],
            device_id={"row": flip(me, d, bits)},
            device_id_type=MESH,
        )

    def first(t):
        src, dst = ((pair, x_all), (cot, ct_all))[t]
        return pltpu.make_async_remote_copy(
            src_ref=src,
            dst_ref=block(dst, me, my_col),
            send_sem=fsend_sem.at[t, 0],
            recv_sem=frecv_sem.at[t, 0],
            device_id={"col": other},
            device_id_type=MESH,
        )

    def forward(t, d):
        ref = (x_all, ct_all)[t]
        held = block(ref, flip(me, d, bits), my_col)
        return pltpu.make_async_remote_copy(
            src_ref=held,
            dst_ref=held,
            send_sem=fsend_sem.at[t, d],
            recv_sem=frecv_sem.at[t, d],
            device_id={"col": other},
            device_id_type=MESH,
        )

    def loop(count, step, start=0):
        def body(k, carry):
            step(k)
            return carry

        lax.fori_loop(start, count, body, 0)

    for t in range(2):
        first(t).start()
        loop(rows, lambda d: direct(t, d).start(), 1)

    for copy in weights:
        copy.wait()
    own[0].wait()

    def rows_of(ref, k0, nk):
        return ref[pl.ds(k0, nk)].reshape(nk * n, c)

    def put(ref, k0, nk, v):
        ref[pl.ds(k0, nk)] = v.reshape(nk, n, c)

    def projected(x, k0, nk, weight, a_ref, b_ref, g_ref):
        y, _ = norm(x)
        p = dot(y, weight)
        m = rows_of(mask, k0, nk)
        put(a_ref, k0, nk, rounded(sigmoid(part(p, 0)) * part(p, 1) * m))
        put(b_ref, k0, nk, rounded(sigmoid(part(p, 2)) * part(p, 3) * m))
        put(g_ref, k0, nk, sigmoid(part(p, 4)))

    def front_step(d):
        @pl.when(d + 1 < rows)
        def _():
            direct(0, d + 1).wait_recv()
            forward(0, d + 1).start()

        forward(0, d).wait_recv()
        k0 = flip(me, d, bits) * lr
        projected(rows_of(x_all, k0, lr).astype(F32), k0, lr, wf[0], left, right, gate)

    loop(rows, front_step)

    def transpose(src):
        def step(b):
            i = pl.multiple_of(b * TILE, TILE)
            flipped[:, pl.ds(i, TILE), :] = jnp.swapaxes(src[pl.ds(i, TILE)], 0, 1)

        loop(n // TILE, step)

    def triangle(count, width, row_at, tile_at, store, group):
        def step(b):
            def term(q, acc):
                t = tile_at(q)
                return tuple(v + row_at(b * group + a, q) * t for a, v in enumerate(acc))

            zero = jnp.zeros((width, c), F32)
            acc = lax.fori_loop(0, n, term, (zero,) * group, unroll=True)
            for a in range(group):
                store(b * group + a, acc[a])

        loop(count // group, step)

    transpose(right)

    def put_row(ref):
        def store(a, v):
            ref[a] = v

        return store

    triangle(
        n, n,
        lambda i, k: left[i, pl.ds(k, 1), :],
        lambda k: flipped[k],
        put_row(mixed), 4,
    )

    own[1].wait()

    def pass_on(d):
        direct(1, d).wait_recv()
        forward(1, d).start()

    loop(rows, pass_on, 1)

    def middle_step(b):
        k0 = b * lr
        z, _ = norm(rows_of(mixed, k0, lr))
        x = rows_of(x_all, k0, lr).astype(F32)
        x = rounded(x + rows_of(gate, k0, lr) * dot(z, wo[0]))
        put(mid, k0, lr, x)
        projected(x, k0, lr, wf[1], in_left, in_right, in_gate)

    loop(rows, middle_step)

    triangle(
        n, n,
        lambda i, k: in_left[k, pl.ds(i, 1), :],
        lambda k: in_right[k],
        put_row(in_mixed), 4,
    )

    loop(rows, lambda d: forward(1, d).wait_recv())

    def signal_step(b):
        k0 = b * lr
        z, r = norm(rows_of(in_mixed, k0, lr))
        ct = rows_of(ct_all, k0, lr).astype(F32)
        put(ct32, k0, lr, ct)
        dz = rounded(dot_t(ct * rows_of(in_gate, k0, lr), wo[1]))
        put(sig, k0, lr, rounded(norm_back(z, r, dz)))

    loop(rows, signal_step)
    transpose(sig)

    def strip(k0, nk, j0, width, group, chunk):
        def take(ref, k, m):
            return ref[pl.ds(k, m), pl.ds(j0, width), :].reshape(m * width, c)

        def give(ref, k, m, v):
            ref[pl.ds(k, m), pl.ds(j0, width), :] = v.reshape(m, width, c)

        def into(ref):
            def store(a, v):
                ref[k0 + a, pl.ds(j0, width), :] = rounded(v)

            return store

        triangle(
            nk, width,
            lambda a, j: in_right[k0 + a, pl.ds(j, 1), :],
            lambda j: flipped[j, pl.ds(j0, width), :],
            into(d_left), group,
        )
        triangle(
            nk, width,
            lambda a, i: in_left[k0 + a, pl.ds(i, 1), :],
            lambda i: sig[i, pl.ds(j0, width), :],
            into(d_right), group,
        )

        def back(b):
            k = k0 + b * chunk
            ct = take(ct32, k, chunk)
            z1, _ = norm(take(in_mixed, k, chunk))
            d_in = front_back(
                take(mid, k, chunk), take(mask, k, chunk), wf[1],
                take(d_left, k, chunk), take(d_right, k, chunk),
                ct * dot(z1, wo[1]),
            )
            g = rounded(ct + d_in)
            z0, r = norm(take(mixed, k, chunk))
            dz = rounded(dot_t(g * take(gate, k, chunk), wo[0]))
            give(grad, k, chunk, g)
            give(out_sig, k, chunk, rounded(norm_back(z0, r, dz)))

        loop(nk // chunk, back)

    t0 = pl.multiple_of(me * lr // TILE * TILE, TILE)
    strip(r0, lr, 0, n, lr, lr)
    strip(0, n, t0, max(TILE, lr), TILE, TILE)

    def own_of(ref):
        def store(a, v):
            ref[r0 + a, pl.ds(c0, lc), :] = rounded(v)

        return store

    triangle(
        lr, lc,
        lambda a, j: out_sig[r0 + a, pl.ds(j, 1), :],
        lambda j: right[j, pl.ds(c0, lc), :],
        own_of(d_left), lr,
    )
    triangle(
        lr, lc,
        lambda a, i: out_sig[i, pl.ds(r0 + a, 1), :],
        lambda i: left[i, pl.ds(c0, lc), :],
        own_of(d_right), lr,
    )

    def mine(ref):
        return ref[pl.ds(r0, lr), pl.ds(c0, lc), :].reshape(lr * lc, c)

    z0, _ = norm(mine(mixed))
    g = mine(grad)
    d_front = front_back(
        mine(x_all).astype(F32), mine(mask), wf[0], mine(d_left), mine(d_right),
        g * dot(z0, wo[0]),
    )
    out[...] = (g + d_front).astype(BF16).reshape(lr, lc, c)

    for t in range(2):
        first(t).wait_send()

        def sent(d):
            direct(t, d).wait_send()
            forward(t, d).wait_send()

        loop(rows, sent, 1)


def from_root(array, axis, root):
    mine = lax.axis_index(axis) == root
    return lax.psum(jnp.where(mine, array, jnp.zeros_like(array)), axis)


def layer_norm(values):
    centred = values - jnp.mean(values, axis=-1, keepdims=True)
    spread = jnp.mean(centred * centred, axis=-1, keepdims=True)
    return centred * lax.rsqrt(spread + 1e-05)


def project_pair(inner_pair, mask_pair, weight):
    normed = layer_norm(inner_pair.astype(jnp.float32)).astype(jnp.bfloat16)
    linear = jnp.dot(normed, weight, preferred_element_type=jnp.float32)
    left_side = jax.nn.sigmoid(linear[..., :H]) * linear[..., H : 2 * H]
    right_side = jax.nn.sigmoid(linear[..., 2 * H : 3 * H]) * linear[..., 3 * H : 4 * H]
    operands = (jnp.stack((left_side, right_side)) * mask_pair[None, :, :, None]).astype(
        jnp.bfloat16
    )
    return (operands, jax.nn.sigmoid(linear[..., 4 * H :]))


def finish(mixed_part, gate_value, inner_pair, weight):
    normed = layer_norm(mixed_part).astype(jnp.bfloat16)
    update = jnp.dot(normed, weight, preferred_element_type=jnp.float32)
    return (inner_pair.astype(jnp.float32) + gate_value * update).astype(jnp.bfloat16)


def body(pair_act, cotangent, residue_mask, front_weight, out_weight):
    local_rows = pair_act.shape[0]
    local_cols = pair_act.shape[1]
    row_index = lax.axis_index("row")
    col_index = lax.axis_index("col")
    block_rows = lax.axis_size("row") // lax.axis_size("col")
    owner_col = row_index // block_rows
    offset = row_index % block_rows * local_rows
    chain_mask = residue_mask.astype(jnp.float32)
    mask_rows = lax.dynamic_slice_in_dim(chain_mask, row_index * local_rows, local_rows)
    mask_cols = lax.dynamic_slice_in_dim(chain_mask, col_index * local_cols, local_cols)
    mask_pair = mask_rows[:, None] * mask_cols[None, :]

    def gather_rows(stacked):
        return lax.all_gather(stacked, "row", axis=1, tiled=True)

    def column_block(gathered):
        slab = lax.dynamic_slice_in_dim(gathered, offset, local_rows, 1)
        return from_root(slab, "col", owner_col)

    def gather_cols(values):
        return lax.all_gather(values, "col", axis=1, tiled=True)

    def sum_cols(partial_term):
        return lax.psum_scatter(
            partial_term.astype(jnp.bfloat16), "col", scatter_dimension=1, tiled=True
        ).astype(jnp.float32)

    (out_ops, out_gate), out_front_back = jax.vjp(
        lambda inner_pair: project_pair(inner_pair, mask_pair, front_weight[0]), pair_act
    )
    fetched = gather_rows(out_ops)
    out_mixed = sum_cols(
        jnp.einsum("ikc,jkc->ijc", out_ops[0], fetched[-1], preferred_element_type=jnp.float32)
    )
    pair_mid, out_finish_back = jax.vjp(
        lambda mixed_part, gate_value, inner_pair: finish(
            mixed_part, gate_value, inner_pair, out_weight[0]
        ),
        out_mixed,
        out_gate,
        pair_act,
    )
    (in_ops, in_gate), in_front_back = jax.vjp(
        lambda inner_pair: project_pair(inner_pair, mask_pair, front_weight[1]), pair_mid
    )
    in_fetched = gather_rows(in_ops)
    left_block = column_block(in_fetched[0])
    in_mixed = jnp.einsum(
        "kic,kjc->ijc", left_block, in_fetched[1], preferred_element_type=jnp.float32
    )
    unused_pair, in_finish_back = jax.vjp(
        lambda mixed_part, gate_value, inner_pair: finish(
            mixed_part, gate_value, inner_pair, out_weight[1]
        ),
        in_mixed,
        in_gate,
        pair_mid,
    )
    grad_mixed, grad_gate, grad_inner = in_finish_back(cotangent)
    signal = grad_mixed.astype(jnp.bfloat16)
    signal_rows = gather_rows(signal[None])[0]
    left_rows = gather_cols(in_ops[0])
    grad_right = jnp.einsum(
        "kic,ijc->kjc", left_rows, signal_rows, preferred_element_type=jnp.float32
    )
    grad_left = sum_cols(
        jnp.einsum("kjc,ijc->kic", in_ops[1], signal_rows, preferred_element_type=jnp.float32)
    )
    (grad_front,) = in_front_back(
        (jnp.stack((grad_left, grad_right)).astype(jnp.bfloat16), grad_gate)
    )
    grad_mid = (grad_inner.astype(jnp.float32) + grad_front.astype(jnp.float32)).astype(
        jnp.bfloat16
    )
    grad_mixed, grad_gate, grad_inner = out_finish_back(grad_mid)
    signal = grad_mixed.astype(jnp.bfloat16)
    signal_cols = gather_cols(signal)
    grad_left = jnp.einsum(
        "ijc,jkc->ikc", signal_cols, fetched[-1], preferred_element_type=jnp.float32
    )
    signal_block = column_block(gather_rows(signal[None])[0])
    grad_right = jnp.einsum(
        "ijc,ikc->jkc", signal_block, fetched[0], preferred_element_type=jnp.float32
    )
    (grad_front,) = out_front_back(
        (jnp.stack((grad_left, grad_right)).astype(jnp.bfloat16), grad_gate)
    )
    return (grad_inner.astype(jnp.float32) + grad_front.astype(jnp.float32)).astype(jnp.bfloat16)


def crop_body(rows, pair_act, cotangent, residue_mask, front_weight, out_weight):
    lr, lc, c = pair_act.shape
    n = residue_mask.shape[0]
    full = pltpu.VMEM((n, n, c), F32)
    dma = pltpu.SemaphoreType.DMA
    hbm = pl.BlockSpec(memory_space=pl.ANY)
    return pl.pallas_call(
        functools.partial(crop_kernel, rows),
        out_shape=jax.ShapeDtypeStruct((lr, lc, c), BF16),
        in_specs=[hbm] * 5,
        out_specs=pl.BlockSpec(memory_space=pltpu.VMEM),
        scratch_shapes=[
            pltpu.VMEM((n, n, c), BF16),
            pltpu.VMEM((n, n, c), BF16),
            pltpu.VMEM(front_weight.shape, BF16),
            pltpu.VMEM(out_weight.shape, BF16),
            pltpu.VMEM((1, n), jnp.int32),
        ]
        + [full] * 17
        + [dma((5,)), dma((2, rows)), dma((2, rows)), dma((2, rows)), dma((2, rows))],
        compiler_params=pltpu.CompilerParams(
            collective_id=0, has_side_effects=True, vmem_limit_bytes=67043328
        ),
    )(pair_act, cotangent, residue_mask.reshape(1, n), front_weight, out_weight)


def fits(mesh, n, lr, lc, c):
    rows, cols = mesh.shape["row"], mesh.shape["col"]
    return (
        cols == 2
        and rows & (rows - 1) == 0
        and n % TILE == 0
        and (lr % TILE == 0 or TILE % lr == 0)
        and lc % (2 * TILE) == 0
        and FULL_ARRAYS * 4 * n * n * c <= VMEM_BUDGET
    )


def solution(mesh):
    def dispatch(pair_act, cotangent, residue_mask, front_weight, out_weight):
        n = residue_mask.shape[0]
        if fits(mesh, n, *pair_act.shape):
            return crop_body(
                mesh.shape["row"], pair_act, cotangent, residue_mask, front_weight, out_weight
            )
        return body(pair_act, cotangent, residue_mask, front_weight, out_weight)

    placed = (P(("grp", "row"), "col", None), P(("grp", "row"), "col", None), P("grp"), P(), P())
    return jax.shard_map(
        dispatch,
        mesh=mesh,
        in_specs=placed,
        out_specs=P(("grp", "row"), "col", None),
        check_vma=False,
    )
```

```python
import functools

import jax
import jax.numpy as jnp
from jax import lax
from jax.experimental import pallas as pl
from jax.experimental.pallas import tpu as pltpu
from jax.sharding import PartitionSpec as P

H = 128
TILE = 8
F32 = jnp.float32
BF16 = jnp.bfloat16
MESH = pl.DeviceIdType.MESH
VMEM_BUDGET = 24 << 20
FULL_ARRAYS = 16


def sigmoid(x):
    return 0.5 * jnp.tanh(0.5 * x) + 0.5


def norm(v):
    centred = v - jnp.mean(v, axis=-1, keepdims=True)
    r = lax.rsqrt(jnp.mean(centred * centred, axis=-1, keepdims=True) + 1e-05)
    return centred * r, r


def norm_back(y, r, d):
    return r * (d - jnp.mean(d, axis=-1, keepdims=True) - y * jnp.mean(d * y, axis=-1, keepdims=True))


def rounded(v):
    return v.astype(BF16).astype(F32)


def dot(a, b):
    return jnp.dot(a.astype(BF16), b, preferred_element_type=F32)


def dot_t(a, b):
    return lax.dot_general(
        a.astype(BF16), b, (((1,), (1,)), ((), ())), preferred_element_type=F32
    )


def part(p, n):
    return p[:, n * H : (n + 1) * H]


def flip(value, other, bits):
    total = 0
    for b in range(bits):
        w = 1 << b
        total = total + (value // w + other // w) % 2 * w
    return total


def front_back(x, mask, weight, d_a, d_b, d_gate):
    y, r = norm(x)
    p = dot(y, weight)
    s0, s2, s4 = sigmoid(part(p, 0)), sigmoid(part(p, 2)), sigmoid(part(p, 4))
    ma, mb = d_a * mask * s0, d_b * mask * s2
    d = jnp.concatenate(
        [
            (v.astype(BF16))
            for v in (
                ma * part(p, 1) * (1.0 - s0),
                ma,
                mb * part(p, 3) * (1.0 - s2),
                mb,
                d_gate * s4 * (1.0 - s4),
            )
        ],
        axis=1,
    )
    return rounded(norm_back(y, r, rounded(dot_t(d, weight))))


def crop_kernel(
    rows, pair, cot, mask_in, wf_in, wo_in, out,
    x_all, ct_all, wf, wo, chain, mask, left, right, flipped, mixed, gate, mid,
    in_left, in_right, in_mixed, in_gate, sig, d_left, d_right, ct32, out_sig, grad,
    local_sem, send_sem, recv_sem, fsend_sem, frecv_sem,
):
    n, c = left.shape[0], left.shape[2]
    lr, lc = out.shape[0], out.shape[1]
    bits = rows.bit_length() - 1
    me, my_col = lax.axis_index("row"), lax.axis_index("col")
    other = 1 - my_col
    r0 = pl.multiple_of(me * lr, lr)
    c0 = pl.multiple_of(my_col * lc, lc)

    weights = [
        pltpu.make_async_copy(wf_in, wf, local_sem.at[2]),
        pltpu.make_async_copy(wo_in, wo, local_sem.at[3]),
    ]
    own = []
    for t, (src, dst) in enumerate(((pair, x_all), (cot, ct_all))):
        own.append(
            pltpu.make_async_copy(src, dst.at[pl.ds(r0, lr), pl.ds(c0, lc)], local_sem.at[t])
        )
    chain_copy = pltpu.make_async_copy(mask_in, chain, local_sem.at[4])
    for copy in [chain_copy] + own + weights:
        copy.start()

    barrier = pltpu.get_barrier_semaphore()
    for d in range(1, rows):
        pl.semaphore_signal(
            barrier, inc=1, device_id={"row": flip(me, d, bits)}, device_id_type=MESH
        )
    pl.semaphore_signal(barrier, inc=1, device_id={"col": other}, device_id_type=MESH)

    chain_copy.wait()
    span = jnp.broadcast_to(chain[...].astype(F32), (n, n))
    here = lax.broadcasted_iota(jnp.int32, (n, n), 0) == lax.broadcasted_iota(jnp.int32, (n, n), 1)
    along = jnp.broadcast_to(
        jnp.sum(jnp.where(here, span, 0.0), axis=1, keepdims=True), (n, c)
    )
    flipped[0] = along

    def fill_mask(i, carry):
        mask[i] = along * flipped[0, pl.ds(i, 1), :]
        return carry

    lax.fori_loop(0, n, fill_mask, 0)
    pl.semaphore_wait(barrier, rows)

    def block(ref, row, col):
        return ref.at[
            pl.ds(pl.multiple_of(row * lr, lr), lr), pl.ds(pl.multiple_of(col * lc, lc), lc)
        ]

    def direct(t, d):
        src, dst = ((pair, x_all), (cot, ct_all))[t]
        return pltpu.make_async_remote_copy(
            src_ref=src,
            dst_ref=block(dst, me, my_col),
            send_sem=send_sem.at[t, d],
            recv_sem=recv_sem.at[t, d],
            device_id={"row": flip(me, d, bits)},
            device_id_type=MESH,
        )

    def first(t):
        src, dst = ((pair, x_all), (cot, ct_all))[t]
        return pltpu.make_async_remote_copy(
            src_ref=src,
            dst_ref=block(dst, me, my_col),
            send_sem=fsend_sem.at[t, 0],
            recv_sem=frecv_sem.at[t, 0],
            device_id={"col": other},
            device_id_type=MESH,
        )

    def forward(t, d):
        ref = (x_all, ct_all)[t]
        held = block(ref, flip(me, d, bits), my_col)
        return pltpu.make_async_remote_copy(
            src_ref=held,
            dst_ref=held,
            send_sem=fsend_sem.at[t, d],
            recv_sem=frecv_sem.at[t, d],
            device_id={"col": other},
            device_id_type=MESH,
        )

    def loop(count, step, start=0):
        def body(k, carry):
            step(k)
            return carry

        lax.fori_loop(start, count, body, 0)

    for t in range(2):
        first(t).start()
        loop(rows, lambda d: direct(t, d).start(), 1)

    for copy in weights:
        copy.wait()
    own[0].wait()

    def rows_of(ref, k0, nk):
        return ref[pl.ds(k0, nk)].reshape(nk * n, c)

    def put(ref, k0, nk, v):
        ref[pl.ds(k0, nk)] = v.reshape(nk, n, c)

    def projected(x, k0, nk, weight, a_ref, b_ref, g_ref):
        y, _ = norm(x)
        p = dot(y, weight)
        m = rows_of(mask, k0, nk)
        put(a_ref, k0, nk, rounded(sigmoid(part(p, 0)) * part(p, 1) * m))
        put(b_ref, k0, nk, rounded(sigmoid(part(p, 2)) * part(p, 3) * m))
        put(g_ref, k0, nk, sigmoid(part(p, 4)))

    def arrived(d):
        direct(0, d).wait_recv()
        forward(0, d).start()

    def front_step(g):
        d = 2 * g

        @pl.when(d + 2 < rows)
        def _():
            arrived(d + 2)
            arrived(d + 3)

        forward(0, d).wait_recv()
        forward(0, d + 1).wait_recv()
        k0 = pl.multiple_of(flip(me, d, bits) // 2 * 2 * lr, 2 * lr)
        projected(rows_of(x_all, k0, 2 * lr).astype(F32), k0, 2 * lr, wf[0], left, right, gate)

    arrived(1)
    loop(rows // 2, front_step)

    def transpose(src):
        def step(b):
            i = pl.multiple_of(b * TILE, TILE)
            flipped[:, pl.ds(i, TILE), :] = jnp.swapaxes(src[pl.ds(i, TILE)], 0, 1)

        loop(n // TILE, step)

    def triangle(count, width, row_at, tile_at, store, group):
        def step(b):
            def term(q, acc):
                t = tile_at(q)
                return tuple(v + row_at(b * group + a, q) * t for a, v in enumerate(acc))

            zero = jnp.zeros((width, c), F32)
            acc = lax.fori_loop(0, n, term, (zero,) * group, unroll=True)
            for a in range(group):
                store(b * group + a, acc[a])

        loop(count // group, step)

    transpose(right)

    def put_row(ref):
        def store(a, v):
            ref[a] = v

        return store

    triangle(
        n, n,
        lambda i, k: left[i, pl.ds(k, 1), :],
        lambda k: flipped[k],
        put_row(mixed), 4,
    )

    own[1].wait()

    def pass_on(d):
        direct(1, d).wait_recv()
        forward(1, d).start()

    loop(rows, pass_on, 1)

    some = min(n, 4 * lr)

    def middle_step(b):
        k0 = b * some
        z, _ = norm(rows_of(mixed, k0, some))
        x = rows_of(x_all, k0, some).astype(F32)
        x = rounded(x + rows_of(gate, k0, some) * dot(z, wo[0]))
        put(mid, k0, some, x)
        projected(x, k0, some, wf[1], in_left, in_right, in_gate)

    loop(n // some, middle_step)

    triangle(
        n, n,
        lambda i, k: in_left[k, pl.ds(i, 1), :],
        lambda k: in_right[k],
        put_row(in_mixed), 4,
    )

    loop(rows, lambda d: forward(1, d).wait_recv())

    def signal_step(b):
        k0 = b * some
        z, r = norm(rows_of(in_mixed, k0, some))
        ct = rows_of(ct_all, k0, some).astype(F32)
        put(ct32, k0, some, ct)
        dz = rounded(dot_t(ct * rows_of(in_gate, k0, some), wo[1]))
        put(sig, k0, some, rounded(norm_back(z, r, dz)))

    loop(n // some, signal_step)
    transpose(sig)

    def strip(k0, nk, j0, width, group, chunk):
        def take(ref, k, m):
            return ref[pl.ds(k, m), pl.ds(j0, width), :].reshape(m * width, c)

        def give(ref, k, m, v):
            ref[pl.ds(k, m), pl.ds(j0, width), :] = v.reshape(m, width, c)

        def into(ref):
            def store(a, v):
                ref[k0 + a, pl.ds(j0, width), :] = rounded(v)

            return store

        triangle(
            nk, width,
            lambda a, j: in_right[k0 + a, pl.ds(j, 1), :],
            lambda j: flipped[j, pl.ds(j0, width), :],
            into(d_left), group,
        )
        triangle(
            nk, width,
            lambda a, i: in_left[k0 + a, pl.ds(i, 1), :],
            lambda i: sig[i, pl.ds(j0, width), :],
            into(d_right), group,
        )

        def back(b):
            k = k0 + b * chunk
            ct = take(ct32, k, chunk)
            z1, _ = norm(take(in_mixed, k, chunk))
            d_in = front_back(
                take(mid, k, chunk), take(mask, k, chunk), wf[1],
                take(d_left, k, chunk), take(d_right, k, chunk),
                ct * dot(z1, wo[1]),
            )
            g = rounded(ct + d_in)
            z0, r = norm(take(mixed, k, chunk))
            dz = rounded(dot_t(g * take(gate, k, chunk), wo[0]))
            give(grad, k, chunk, g)
            give(out_sig, k, chunk, rounded(norm_back(z0, r, dz)))

        loop(nk // chunk, back)

    t0 = pl.multiple_of(me * lr // TILE * TILE, TILE)
    strip(r0, lr, 0, n, lr, lr)
    strip(0, n, t0, max(TILE, lr), TILE, 4 * TILE if n % (4 * TILE) == 0 else TILE)

    def own_of(ref):
        def store(a, v):
            ref[r0 + a, pl.ds(c0, lc), :] = rounded(v)

        return store

    triangle(
        lr, lc,
        lambda a, j: out_sig[r0 + a, pl.ds(j, 1), :],
        lambda j: right[j, pl.ds(c0, lc), :],
        own_of(d_left), lr,
    )
    triangle(
        lr, lc,
        lambda a, i: out_sig[i, pl.ds(r0 + a, 1), :],
        lambda i: left[i, pl.ds(c0, lc), :],
        own_of(d_right), lr,
    )

    def mine(ref):
        return ref[pl.ds(r0, lr), pl.ds(c0, lc), :].reshape(lr * lc, c)

    z0, _ = norm(mine(mixed))
    g = mine(grad)
    d_front = front_back(
        mine(x_all).astype(F32), mine(mask), wf[0], mine(d_left), mine(d_right),
        g * dot(z0, wo[0]),
    )
    out[...] = (g + d_front).astype(BF16).reshape(lr, lc, c)

    for t in range(2):
        first(t).wait_send()

        def sent(d):
            direct(t, d).wait_send()
            forward(t, d).wait_send()

        loop(rows, sent, 1)


def from_root(array, axis, root):
    mine = lax.axis_index(axis) == root
    return lax.psum(jnp.where(mine, array, jnp.zeros_like(array)), axis)


def layer_norm(values):
    centred = values - jnp.mean(values, axis=-1, keepdims=True)
    spread = jnp.mean(centred * centred, axis=-1, keepdims=True)
    return centred * lax.rsqrt(spread + 1e-05)


def project_pair(inner_pair, mask_pair, weight):
    normed = layer_norm(inner_pair.astype(jnp.float32)).astype(jnp.bfloat16)
    linear = jnp.dot(normed, weight, preferred_element_type=jnp.float32)
    left_side = jax.nn.sigmoid(linear[..., :H]) * linear[..., H : 2 * H]
    right_side = jax.nn.sigmoid(linear[..., 2 * H : 3 * H]) * linear[..., 3 * H : 4 * H]
    operands = (jnp.stack((left_side, right_side)) * mask_pair[None, :, :, None]).astype(
        jnp.bfloat16
    )
    return (operands, jax.nn.sigmoid(linear[..., 4 * H :]))


def finish(mixed_part, gate_value, inner_pair, weight):
    normed = layer_norm(mixed_part).astype(jnp.bfloat16)
    update = jnp.dot(normed, weight, preferred_element_type=jnp.float32)
    return (inner_pair.astype(jnp.float32) + gate_value * update).astype(jnp.bfloat16)


def body(pair_act, cotangent, residue_mask, front_weight, out_weight):
    local_rows = pair_act.shape[0]
    local_cols = pair_act.shape[1]
    row_index = lax.axis_index("row")
    col_index = lax.axis_index("col")
    block_rows = lax.axis_size("row") // lax.axis_size("col")
    owner_col = row_index // block_rows
    offset = row_index % block_rows * local_rows
    chain_mask = residue_mask.astype(jnp.float32)
    mask_rows = lax.dynamic_slice_in_dim(chain_mask, row_index * local_rows, local_rows)
    mask_cols = lax.dynamic_slice_in_dim(chain_mask, col_index * local_cols, local_cols)
    mask_pair = mask_rows[:, None] * mask_cols[None, :]

    def gather_rows(stacked):
        return lax.all_gather(stacked, "row", axis=1, tiled=True)

    def column_block(gathered):
        slab = lax.dynamic_slice_in_dim(gathered, offset, local_rows, 1)
        return from_root(slab, "col", owner_col)

    def gather_cols(values):
        return lax.all_gather(values, "col", axis=1, tiled=True)

    def sum_cols(partial_term):
        return lax.psum_scatter(
            partial_term.astype(jnp.bfloat16), "col", scatter_dimension=1, tiled=True
        ).astype(jnp.float32)

    (out_ops, out_gate), out_front_back = jax.vjp(
        lambda inner_pair: project_pair(inner_pair, mask_pair, front_weight[0]), pair_act
    )
    fetched = gather_rows(out_ops)
    out_mixed = sum_cols(
        jnp.einsum("ikc,jkc->ijc", out_ops[0], fetched[-1], preferred_element_type=jnp.float32)
    )
    pair_mid, out_finish_back = jax.vjp(
        lambda mixed_part, gate_value, inner_pair: finish(
            mixed_part, gate_value, inner_pair, out_weight[0]
        ),
        out_mixed,
        out_gate,
        pair_act,
    )
    (in_ops, in_gate), in_front_back = jax.vjp(
        lambda inner_pair: project_pair(inner_pair, mask_pair, front_weight[1]), pair_mid
    )
    in_fetched = gather_rows(in_ops)
    left_block = column_block(in_fetched[0])
    in_mixed = jnp.einsum(
        "kic,kjc->ijc", left_block, in_fetched[1], preferred_element_type=jnp.float32
    )
    unused_pair, in_finish_back = jax.vjp(
        lambda mixed_part, gate_value, inner_pair: finish(
            mixed_part, gate_value, inner_pair, out_weight[1]
        ),
        in_mixed,
        in_gate,
        pair_mid,
    )
    grad_mixed, grad_gate, grad_inner = in_finish_back(cotangent)
    signal = grad_mixed.astype(jnp.bfloat16)
    signal_rows = gather_rows(signal[None])[0]
    left_rows = gather_cols(in_ops[0])
    grad_right = jnp.einsum(
        "kic,ijc->kjc", left_rows, signal_rows, preferred_element_type=jnp.float32
    )
    grad_left = sum_cols(
        jnp.einsum("kjc,ijc->kic", in_ops[1], signal_rows, preferred_element_type=jnp.float32)
    )
    (grad_front,) = in_front_back(
        (jnp.stack((grad_left, grad_right)).astype(jnp.bfloat16), grad_gate)
    )
    grad_mid = (grad_inner.astype(jnp.float32) + grad_front.astype(jnp.float32)).astype(
        jnp.bfloat16
    )
    grad_mixed, grad_gate, grad_inner = out_finish_back(grad_mid)
    signal = grad_mixed.astype(jnp.bfloat16)
    signal_cols = gather_cols(signal)
    grad_left = jnp.einsum(
        "ijc,jkc->ikc", signal_cols, fetched[-1], preferred_element_type=jnp.float32
    )
    signal_block = column_block(gather_rows(signal[None])[0])
    grad_right = jnp.einsum(
        "ijc,ikc->jkc", signal_block, fetched[0], preferred_element_type=jnp.float32
    )
    (grad_front,) = out_front_back(
        (jnp.stack((grad_left, grad_right)).astype(jnp.bfloat16), grad_gate)
    )
    return (grad_inner.astype(jnp.float32) + grad_front.astype(jnp.float32)).astype(jnp.bfloat16)


def crop_body(rows, pair_act, cotangent, residue_mask, front_weight, out_weight):
    lr, lc, c = pair_act.shape
    n = residue_mask.shape[0]
    full = pltpu.VMEM((n, n, c), F32)
    dma = pltpu.SemaphoreType.DMA
    hbm = pl.BlockSpec(memory_space=pl.ANY)
    return pl.pallas_call(
        functools.partial(crop_kernel, rows),
        out_shape=jax.ShapeDtypeStruct((lr, lc, c), BF16),
        in_specs=[hbm] * 5,
        out_specs=pl.BlockSpec(memory_space=pltpu.VMEM),
        scratch_shapes=[
            pltpu.VMEM((n, n, c), BF16),
            pltpu.VMEM((n, n, c), BF16),
            pltpu.VMEM(front_weight.shape, BF16),
            pltpu.VMEM(out_weight.shape, BF16),
            pltpu.VMEM((1, n), jnp.int32),
        ]
        + [full] * 17
        + [dma((5,)), dma((2, rows)), dma((2, rows)), dma((2, rows)), dma((2, rows))],
        compiler_params=pltpu.CompilerParams(
            collective_id=0, has_side_effects=True, vmem_limit_bytes=67043328
        ),
    )(pair_act, cotangent, residue_mask.reshape(1, n), front_weight, out_weight)


def fits(mesh, n, lr, lc, c):
    rows, cols = mesh.shape["row"], mesh.shape["col"]
    return (
        cols == 2
        and rows >= 2
        and rows & (rows - 1) == 0
        and n % TILE == 0
        and (lr % TILE == 0 or TILE % lr == 0)
        and lc % (2 * TILE) == 0
        and FULL_ARRAYS * 4 * n * n * c <= VMEM_BUDGET
    )


def solution(mesh):
    def dispatch(pair_act, cotangent, residue_mask, front_weight, out_weight):
        n = residue_mask.shape[0]
        if fits(mesh, n, *pair_act.shape):
            return crop_body(
                mesh.shape["row"], pair_act, cotangent, residue_mask, front_weight, out_weight
            )
        return body(pair_act, cotangent, residue_mask, front_weight, out_weight)

    placed = (P(("grp", "row"), "col", None), P(("grp", "row"), "col", None), P("grp"), P(), P())
    return jax.shard_map(
        dispatch,
        mesh=mesh,
        in_specs=placed,
        out_specs=P(("grp", "row"), "col", None),
        check_vma=False,
    )
```
